256 devices in a mesh: smp: 32 (over x_lo, z, core), par: 8 (over x_hi, y).
Axes of the slice: x: 4 (x_hi: 2, x_lo: 2; x = x_hi * 2 + x_lo), y: 4, z: 8, core: 2. Of those that a mesh axis runs over, the one named last changes fastest.
Arguments:
- log_derivs: float32 [8192, 8192], P('smp', 'par'), may hold values from -40 to 40, as said below
- coefficients: float32 [8192], P('smp'), may hold values from -6 to 6
Outputs:
- gram: float32 [8192, 8192], P('smp', 'par')
- update: float32 [8192], P(('par', 'smp'))
The draws below stay inside these ranges and needn't reach their ends.
Inputs may be any that keep to these rules, and one draw needn't show every extreme that they name: `log_derivs`: finite real values.
All inputs are finite; a program needn't handle non-finite values.
Results may differ from the reference program's by a relative error of at most 0.00014.
Values sent between devices are 32-bit elements; how exact they have to be, the bound alone decides.
A program may use at most 128 MiB of HBM per device.

```python
import jax
import jax.numpy as jnp
from jax import lax

SAMPLES = 8192
PARAMS = 8192


def draw_log_derivs(key, part):
    keys_split = jax.random.split(jax.random.fold_in(key, 17), 4)
    column_offset = jax.random.uniform(keys_split[0], (PARAMS,), jnp.float32, -1.5, 1.5)
    sample_ramp = 1.0 + 2.0 * jnp.arange(SAMPLES, dtype=jnp.float32) / SAMPLES
    row_scale = jnp.exp(jax.random.uniform(keys_split[1], (SAMPLES, 1), jnp.float32, 0.0, 1.0986))
    column_scale = jnp.exp(jax.random.uniform(keys_split[2], (1, PARAMS), jnp.float32, 0.0, 1.0986))
    noise = jnp.clip(jax.random.normal(keys_split[3], (SAMPLES, PARAMS), jnp.float32), -4.0, 4.0)
    values = column_offset[None, :] * sample_ramp[:, None] + 0.8 * row_scale * column_scale * noise
    return values.astype(jnp.float32)


def steps_of(key, shape, cuts, smallest, top_value):
    factor_of, own = 1.0, jax.random.fold_in(key, 6)
    for axis_at, blocks in cuts:
        draws = jnp.exp(jax.random.uniform(jax.random.fold_in(own, axis_at), (blocks,), jnp.float32, smallest / len(cuts), top_value / len(cuts)))
        factor_of = factor_of * jnp.repeat(draws, shape[axis_at] // blocks).reshape([-1 if axis == axis_at else 1 for axis in range(len(shape))])
    return factor_of


def normal_values(rng, shape, width, limit, shards=(), kind=jnp.bfloat16):
    values = jax.random.normal(rng, shape, jnp.float32) * width
    if len(shards) > 0:
        values = steps_of(rng, shape, shards, -0.22, 0.18) * values
    return jnp.clip(values, min=-limit, max=limit).astype(kind)


def setup_inputs(seed: int = 0) -> dict:
    key_of = jax.random.split(jax.random.key(seed), 3)
    return {
        "log_derivs": draw_log_derivs(jax.random.fold_in(key_of[2], 71), 0),
        "coefficients": normal_values(key_of[1], (SAMPLES,), 1.0, 6.0, ((0, 32),), jnp.float32),
    }


def reference(log_derivs, coefficients):
    column_mean = lax.optimization_barrier(jnp.sum(log_derivs, axis=0)) / SAMPLES
    centred = (log_derivs - column_mean[None, :]) / jnp.sqrt(jnp.float32(SAMPLES))
    gram = jnp.dot(centred, centred.T, precision=lax.Precision.HIGHEST, preferred_element_type=jnp.float32)
    update = jnp.dot(coefficients, centred, precision=lax.Precision.HIGHEST, preferred_element_type=jnp.float32)
    return (gram, update)
```

```python
import functools

import jax
import jax.numpy as jnp
from jax import lax
from jax.experimental import pallas as pl
from jax.experimental.pallas import tpu as pltpu
from jax.sharding import PartitionSpec as P

MESH = pl.DeviceIdType.MESH
NZ, NY = 8, 4
BLOCKS = 8
CHUNKS = 16
CHUNK_ROWS, LANES = 64, 128
STEPS = BLOCKS * CHUNKS
LAG = 4
LATE = 7 * LAG
COMPUTE_AT = CHUNKS + LATE + 8
COMPUTE_END = COMPUTE_AT + BLOCKS * CHUNKS


def merge(stats):
    count = stats.shape[0]
    mean = jnp.sum(stats[:, 0:1, :], axis=0) * (1.0 / count)
    shift = stats[:, 0:1, :] - mean[None]
    update = jnp.sum(stats[:, 1:2, :] + stats[:, 2:3, :] * shift, axis=0)
    weight = jnp.sum(stats[:, 2:3, :], axis=0)
    return mean, update, weight


def split(values):
    high = values.astype(jnp.bfloat16)
    low = (values - high.astype(jnp.float32)).astype(jnp.bfloat16)
    return high, low


def product(left, right):
    return lax.dot_general(left, right, (((1,), (1,)), ((), ())), preferred_element_type=jnp.float32)


def kernel(
    x_ref, coef_ref, gram_ref, update_ref,
    rows, cols, part, landed, row_hi, row_lo, col_hi, col_lo, near, ring, means,
    load_sem, near_send, near_recv, ring_send, ring_recv, mean_send, mean_recv,
    row_send, row_recv, half_send, half_recv, share_send,
    send, recv, extra_send, extra_recv, part_send, part_recv,
):
    smp, par = lax.axis_index("smp"), lax.axis_index("par")
    core, z, xl = lax.rem(smp, 2), lax.rem(smp // 2, NZ), smp // (2 * NZ)
    y, xh = lax.rem(par, NY), par // NY
    h = lax.rem(z - 2 * y + NZ, NZ)

    def at(dz=0, dy=0, dc=0, dxl=0, dxh=0):
        zz, yy = lax.rem(z + dz + NZ, NZ), lax.rem(y + dy + NY, NY)
        cc, ll, hh = lax.rem(core + dc, 2), lax.rem(xl + dxl, 2), lax.rem(xh + dxh, 2)
        return {"smp": (ll * NZ + zz) * 2 + cc, "par": hh * NY + yy}

    def remote(src, dst, s_sem, r_sem, device):
        return pltpu.make_async_remote_copy(
            src_ref=src, dst_ref=dst, send_sem=s_sem, recv_sem=r_sem, device_id=device, device_id_type=MESH
        )

    load = pltpu.make_async_copy(x_ref, rows.at[0], load_sem)
    load.start()
    barrier = pltpu.get_barrier_semaphore()
    for dz in range(1, NZ):
        pl.semaphore_signal(barrier, inc=1, device_id=at(dz=dz), device_id_type=MESH)
    for dy in range(1, NY):
        pl.semaphore_signal(barrier, inc=1, device_id=at(dy=dy), device_id_type=MESH)
    for b in range(1, 8):
        pl.semaphore_signal(barrier, inc=1, device_id=at(dc=b % 2, dxl=b // 2 % 2, dxh=b // 4), device_id_type=MESH)
    load.wait()
    x = rows[0]
    mean = jnp.sum(x, axis=0, keepdims=True) * (1.0 / x.shape[0])
    coef = coef_ref[...]
    weighted = lax.dot_general(
        jnp.broadcast_to(coef, (8, coef.shape[1])), x - mean, (((1,), (0,)), ((), ())),
        precision=lax.Precision.HIGHEST, preferred_element_type=jnp.float32,
    )
    weight = jnp.broadcast_to(jnp.sum(coef, axis=1, keepdims=True), mean.shape)
    near[0, 0:1, :] = mean
    near[0, 1:2, :] = weighted[0:1, :]
    near[0, 2:3, :] = weight
    near[0, 3:4, :] = weight
    pl.semaphore_wait(barrier, NZ + NY + 8 - 3)

    near_copies = [
        remote(near.at[0], near.at[b], near_send.at[b - 1], near_recv.at[b - 1], at(dc=b % 2, dxl=b // 2))
        for b in range(1, 4)
    ]
    ring_copies = [
        remote(ring.at[0], ring.at[NZ - dz], ring_send.at[dz - 1], ring_recv.at[NZ - dz - 1], at(dz=dz))
        for dz in range(1, NZ)
    ]
    mean_copies = [
        remote(means.at[0], means.at[slot], mean_send.at[slot - 1], mean_recv.at[slot - 1], at(dy=dy))
        for slot, dy in ((2, 1), (1, -1), (3, 2))
    ]

    def to_up(g):
        return remote(rows.at[8 * g], rows.at[8 * g + 2], row_send.at[4 * g], row_recv.at[4 * g + 2], at(dy=1))

    def to_down(g):
        return remote(rows.at[8 * g], rows.at[8 * g + 1], row_send.at[4 * g + 1], row_recv.at[4 * g + 1], at(dy=-1))

    def half_down(g):
        top = pl.ds(0, 128)
        return remote(rows.at[8 * g + 1, top], rows.at[8 * g + 3, top], half_send.at[2 * g], half_recv.at[2 * g], at(dy=-1))

    def half_up(g):
        low = pl.ds(128, 128)
        return remote(rows.at[8 * g + 2, low], rows.at[8 * g + 3, low], half_send.at[2 * g + 1], half_recv.at[2 * g + 1], at(dy=1))

    def across():
        return remote(rows.at[0], rows.at[8], row_send.at[2], row_recv.at[0], at(dxl=1))

    def share(g, j):
        slot = 4 * g + j
        return remote(rows.at[8 * g + j], rows.at[8 * g + 4 + j], share_send.at[slot], row_recv.at[8 + slot], at(dc=1))

    for copy in near_copies:
        copy.start()
    across().start()
    to_up(0).start()
    to_down(0).start()
    share(0, 0).start()
    for copy in near_copies:
        copy.wait_recv()
    merged = merge(near[...])
    for row, value in enumerate(merged + (merged[2],)):
        ring[0, row : row + 1, :] = value
    for copy in ring_copies:
        copy.start()

    places = (h, lax.rem(9 - h, NZ))

    def piece(direction, idx):
        i, r = idx // CHUNKS, lax.rem(idx, CHUNKS)
        chunk_rows = pl.ds(pl.multiple_of(128 * direction + CHUNK_ROWS * lax.rem(r, 2), CHUNK_ROWS), CHUNK_ROWS)
        lanes = pl.ds(pl.multiple_of(LANES * (r // 2), LANES), LANES)
        return i, chunk_rows, lanes

    def chunk_copy(direction, idx, own):
        i, chunk_rows, lanes = piece(direction, idx)
        src = rows.at[i // 2] if own else cols.at[i]
        return remote(
            src.at[chunk_rows, lanes], cols.at[i, chunk_rows, lanes],
            send.at[direction, idx], recv.at[direction, idx], at(dz=1 - 2 * direction),
        )

    def extra_copy(direction, j, q):
        i = 2 * j + (1 - direction)
        half, lanes = pl.ds(128 * direction, 128), pl.ds(pl.multiple_of(256 * q, 256), 256)
        return remote(
            rows.at[j, half, lanes], cols.at[i, half, lanes],
            extra_send.at[direction, 4 * j + q], extra_recv.at[direction, 4 * j + q], at(dz=2 * direction - 1),
        )

    def source_of(direction, idx):
        e = lax.rem(idx // CHUNKS, 2)
        return e if direction == 0 else 1 - e

    def stream(n):
        for direction in range(2):
            place = places[direction]
            idx = n - place * LAG

            @pl.when(jnp.logical_and(idx >= 0, idx < STEPS))
            def _():
                source = source_of(direction, idx)

                @pl.when(place == source)
                def _():
                    chunk_copy(direction, idx, True).start()

                    @pl.when(jnp.logical_and(place == 1, lax.rem(idx, 4) == 3))
                    def _():
                        extra_copy(direction, idx // (2 * CHUNKS), lax.rem(idx, CHUNKS) // 4).start()

                @pl.when(jnp.logical_and(place != source, place >= 1))
                def _():
                    copy = chunk_copy(direction, idx, False)
                    copy.wait_recv()

                    @pl.when(place <= 6)
                    def _():
                        copy.start()

    def serve(n):
        @pl.when(n == 12)
        def _():
            for copy in ring_copies:
                copy.wait_recv()
            mean, update, weight = merge(ring[...])
            for row, value in enumerate((mean, update, weight, weight)):
                means[0, row : row + 1, :] = value
            update_ref[...] = update * (1.0 / 8192.0**0.5)
            for copy in mean_copies:
                copy.start()

        @pl.when(n == 2 * CHUNKS)
        def _():
            to_down(0).wait_recv()
            to_up(0).wait_recv()
            half_down(0).start()
            half_up(0).start()
            share(0, 1).start()
            share(0, 2).start()
            across().wait_recv()
            to_up(1).start()
            to_down(1).start()
            share(1, 0).start()

        @pl.when(n == 2 * CHUNKS + 8)
        def _():
            for copy in mean_copies:
                copy.wait_recv()

        @pl.when(n == 4 * CHUNKS)
        def _():
            half_down(0).wait_recv()
            half_up(0).wait_recv()
            share(0, 3).start()

        @pl.when(n == COMPUTE_AT + 2 * CHUNKS - 4)
        def _():
            to_down(1).wait_recv()
            to_up(1).wait_recv()
            half_down(1).start()
            half_up(1).start()
            share(1, 1).start()
            share(1, 2).start()

        @pl.when(n == COMPUTE_AT + 4 * CHUNKS - 12)
        def _():
            half_down(1).wait_recv()
            half_up(1).wait_recv()
            share(1, 3).start()

    def compute(n):
        t = n - COMPUTE_AT
        i, r = t // CHUNKS, lax.rem(t, CHUNKS)
        e, j = lax.rem(i, 2), i // 2

        @pl.when(jnp.logical_and(t >= 0, r == 0))
        def _():
            @pl.when(e == 0)
            def _():
                share(0, j).wait_recv()
                share(1, j).wait_recv()

            for direction in range(2):
                @pl.when(jnp.logical_and(places[direction] == 0, e == 1 - direction))
                def _():
                    for q in range(4):
                        extra_copy(direction, j, q).wait_recv()

            def convert(block):
                high, low = split(block - means[j, 0:1, :])
                col_hi[...] = high
                col_lo[...] = low

            @pl.when(h == e)
            def _():
                convert(rows[j])

            @pl.when(h != e)
            def _():
                convert(cols[i])

        @pl.when(jnp.logical_and(t >= 0, lax.rem(r, 2) == 0))
        def _():
            k = r // 2
            inner = pl.ds(pl.multiple_of(128 * lax.rem(k, 2), 128), 128)
            high, low = split(rows[4 * (k // 2) + j, inner, :] - means[j, 0:1, :])
            row_hi[...] = high
            row_lo[...] = low
            total = product(row_hi[...], col_hi[...])
            total += product(row_hi[...], col_lo[...])
            total += product(row_lo[...], col_hi[...])
            out = pl.ds(pl.multiple_of(128 * k, 128), 128)

            @pl.when(j == 0)
            def _():
                part[e, out, :] = total

            @pl.when(j != 0)
            def _():
                part[e, out, :] += total

    def part_copy(e, g, c):
        k = 2 * g + c
        slot = 4 * e + 2 * xh + core
        device = {"smp": (lax.rem(xl + g, 2) * NZ + z) * 2 + lax.rem(core + c, 2), "par": xl * NY + y}
        return remote(part.at[e, pl.ds(256 * k, 256)], landed.at[slot], part_send.at[4 * e + k], part_recv.at[slot], device)

    def hand_out(e):
        for g, c in ((1, 0), (1, 1), (0, 1)):
            part_copy(e, g, c).start()

        @pl.when(xl == xh)
        def _():
            landed[4 * e + 2 * xh + core] = part[e, 0:256, :]

        @pl.when(xl != xh)
        def _():
            part_copy(e, 0, 0).start()

    @pl.loop(0, STEPS + LATE)
    def _(n):
        serve(n)
        stream(n)
        compute(n)

    @pl.loop(STEPS + LATE, COMPUTE_END - CHUNKS)
    def _(n):
        compute(n)

    hand_out(0)

    @pl.loop(COMPUTE_END - CHUNKS, COMPUTE_END)
    def _(n):
        compute(n)

    hand_out(1)

    for copy in near_copies + ring_copies + mean_copies:
        copy.wait_send()
    for copy in (across(), to_up(0), to_down(0), to_up(1), to_down(1), half_down(0), half_up(0), half_down(1), half_up(1)):
        copy.wait_send()
    for g in range(2):
        for j in range(4):
            share(g, j).wait_send()

    @pl.loop(0, STEPS)
    def _(idx):
        for direction in range(2):
            place = places[direction]
            source = source_of(direction, idx)

            @pl.when(jnp.logical_or(place == source, jnp.logical_and(place >= 1, place <= 6)))
            def _():
                chunk_copy(direction, idx, False).wait_send()

    for direction in range(2):
        @pl.when(places[direction] == 1)
        def _():
            @pl.loop(0, 16)
            def _(q):
                extra_copy(direction, q // 4, lax.rem(q, 4)).wait_send()

    for e in range(2):
        for source_xh in range(2):
            for source_core in range(2):
                slot = 4 * e + 2 * source_xh + source_core
                own = jnp.logical_and(jnp.logical_and(xl == xh, xh == source_xh), core == source_core)

                @pl.when(jnp.logical_not(own))
                def _():
                    remote(part.at[0, pl.ds(0, 256)], landed.at[slot], part_send.at[0], part_recv.at[slot], at(dc=1)).wait_recv()

        for source_core in range(2):
            gram_ref[:, 256 * (2 * e + source_core) : 256 * (2 * e + source_core + 1)] = (
                landed[4 * e + source_core] + landed[4 * e + 2 + source_core]
            ) * (1.0 / 8192.0)

    for e in range(2):
        for g, c in ((1, 0), (1, 1), (0, 1)):
            part_copy(e, g, c).wait_send()

        @pl.when(xl != xh)
        def _():
            part_copy(e, 0, 0).wait_send()


def local(log_derivs, coefficients):
    count, width = log_derivs.shape
    dma = pltpu.SemaphoreType.DMA
    f32, bf16 = jnp.float32, jnp.bfloat16
    gram, update = pl.pallas_call(
        kernel,
        out_shape=(jax.ShapeDtypeStruct((count, width), f32), jax.ShapeDtypeStruct((1, width), f32)),
        in_specs=[pl.BlockSpec(memory_space=pl.ANY), pl.BlockSpec(memory_space=pltpu.VMEM)],
        out_specs=(pl.BlockSpec(memory_space=pltpu.VMEM), pl.BlockSpec(memory_space=pltpu.VMEM)),
        scratch_shapes=[
            pltpu.VMEM((16, count, width), f32),
            pltpu.VMEM((BLOCKS, count, width), f32),
            pltpu.VMEM((2, 4 * count, count), f32),
            pltpu.VMEM((8, count, count), f32),
            pltpu.VMEM((128, width), bf16),
            pltpu.VMEM((128, width), bf16),
            pltpu.VMEM((count, width), bf16),
            pltpu.VMEM((count, width), bf16),
            pltpu.VMEM((4, 4, width), f32),
            pltpu.VMEM((NZ, 4, width), f32),
            pltpu.VMEM((NY, 4, width), f32),
            dma(()), dma((3,)), dma((3,)), dma((NZ - 1,)), dma((NZ - 1,)), dma((3,)), dma((3,)),
            dma((8,)), dma((16,)), dma((4,)), dma((4,)), dma((8,)),
            dma((2, STEPS)), dma((2, STEPS)), dma((2, 16)), dma((2, 16)), dma((8,)), dma((8,)),
        ],
        compiler_params=pltpu.CompilerParams(collective_id=0, has_side_effects=True, vmem_limit_bytes=60 * 2**20),
    )(log_derivs, coefficients.reshape(1, count))
    start = lax.axis_index("smp") * (width // lax.axis_size("smp"))
    return gram, lax.dynamic_slice(update.reshape(width), (start,), (width // lax.axis_size("smp"),))


def solution(mesh):
    placed = (P("smp", "par"), P("smp"))
    return jax.shard_map(
        local,
        mesh=mesh,
        in_specs=placed,
        out_specs=(P("smp", "par"), P(("par", "smp"))),
        check_vma=False,
    )
```

```python
import functools

import jax
import jax.numpy as jnp
from jax import lax
from jax.experimental import pallas as pl
from jax.experimental.pallas import tpu as pltpu
from jax.sharding import PartitionSpec as P

MESH = pl.DeviceIdType.MESH
NZ, NY = 8, 4
UNITS = 16
CHUNK_ROWS = 16
CHUNKS = 128 // CHUNK_ROWS
STEPS = UNITS * CHUNKS
HOP = 5
COMPUTE_AT = 38
EARLY = 8


def merge(stats):
    count = stats.shape[0]
    mean = jnp.sum(stats[:, 0:1, :], axis=0) * (1.0 / count)
    shift = stats[:, 0:1, :] - mean[None]
    update = jnp.sum(stats[:, 1:2, :] + stats[:, 2:3, :] * shift, axis=0)
    weight = jnp.sum(stats[:, 2:3, :], axis=0)
    return mean, update, weight


def split(values):
    high = values.astype(jnp.bfloat16)
    low = (values - high.astype(jnp.float32)).astype(jnp.bfloat16)
    return high, low


def product(left, right):
    return lax.dot_general(left, right, (((1,), (1,)), ((), ())), preferred_element_type=jnp.float32)


def kernel(
    x_ref, coef_ref, gram_ref, update_ref,
    rows, cols, part, landed, row_hi, row_lo, col_hi, col_lo, near, ring, means,
    load_sem, near_send, near_recv, ring_send, ring_recv, mean_send, mean_recv,
    row_send, row_recv, half_send, half_recv, share_send, send, recv, part_send, part_recv,
):
    smp, par = lax.axis_index("smp"), lax.axis_index("par")
    core, z, xl = lax.rem(smp, 2), lax.rem(smp // 2, NZ), smp // (2 * NZ)
    y, xh = lax.rem(par, NY), par // NY
    place = lax.rem((1 - 2 * core) * (z - 2 * y - 1) + 3 * NZ - core, NZ)
    onward = 1 - 2 * core
    relay = (place + 7) // 8
    behind = HOP * (place - 6 * (place // 7))

    def at(dz=0, dy=0, dc=0, dxl=0, dxh=0):
        zz, yy = lax.rem(z + dz + NZ, NZ), lax.rem(y + dy + NY, NY)
        cc, ll, hh = lax.rem(core + dc, 2), lax.rem(xl + dxl, 2), lax.rem(xh + dxh, 2)
        return {"smp": (ll * NZ + zz) * 2 + cc, "par": hh * NY + yy}

    def remote(src, dst, s_sem, r_sem, device):
        return pltpu.make_async_remote_copy(
            src_ref=src, dst_ref=dst, send_sem=s_sem, recv_sem=r_sem, device_id=device, device_id_type=MESH
        )

    load = pltpu.make_async_copy(x_ref, rows.at[0], load_sem)
    load.start()
    barrier = pltpu.get_barrier_semaphore()
    for dz in range(1, NZ):
        pl.semaphore_signal(barrier, inc=1, device_id=at(dz=dz), device_id_type=MESH)
    for dy in range(1, NY):
        pl.semaphore_signal(barrier, inc=1, device_id=at(dy=dy), device_id_type=MESH)
    for b in range(1, 8):
        pl.semaphore_signal(barrier, inc=1, device_id=at(dc=b % 2, dxl=b // 2 % 2, dxh=b // 4), device_id_type=MESH)
    load.wait()
    pl.semaphore_wait(barrier, NZ + NY + 8 - 3)

    near_copies = [
        remote(near.at[0], near.at[b], near_send.at[b - 1], near_recv.at[b - 1], at(dc=b % 2, dxl=b // 2))
        for b in range(1, 4)
    ]
    ring_copies = [
        remote(ring.at[0], ring.at[NZ - dz], ring_send.at[dz - 1], ring_recv.at[NZ - dz - 1], at(dz=dz))
        for dz in range(1, NZ)
    ]
    mean_copies = [
        remote(means.at[0], means.at[slot], mean_send.at[slot - 1], mean_recv.at[slot - 1], at(dy=dy))
        for slot, dy in ((2, 1), (1, -1), (3, 2))
    ]

    def to_up(g):
        return remote(rows.at[8 * g], rows.at[8 * g + 2], row_send.at[4 * g], row_recv.at[4 * g + 2], at(dy=1))

    def to_down(g):
        return remote(rows.at[8 * g], rows.at[8 * g + 1], row_send.at[4 * g + 1], row_recv.at[4 * g + 1], at(dy=-1))

    def half_down(g):
        top = pl.ds(0, 128)
        return remote(rows.at[8 * g + 1, top], rows.at[8 * g + 3, top], half_send.at[2 * g], half_recv.at[2 * g], at(dy=-1))

    def half_up(g):
        low = pl.ds(128, 128)
        return remote(rows.at[8 * g + 2, low], rows.at[8 * g + 3, low], half_send.at[2 * g + 1], half_recv.at[2 * g + 1], at(dy=1))

    def across():
        return remote(rows.at[0], rows.at[8], row_send.at[2], row_recv.at[0], at(dxl=1))

    def share(g, j):
        slot = 4 * g + j
        return remote(rows.at[8 * g + j], rows.at[8 * g + 4 + j], share_send.at[slot], row_recv.at[8 + slot], at(dc=1))

    def unit(u):
        q, v = u // 4, lax.rem(u, 4)
        third, fourth = (q // 2) * (1 - lax.rem(q, 2)), (q // 2) * lax.rem(q, 2)
        first = 1 - q // 2
        j = first * q + third * (2 + v // 2) + fourth * (2 + lax.rem(v, 2))
        f = first * v + third * lax.rem(v, 2) + fourth * (2 + v // 2)
        return j, f

    def home(j, f):
        return 4 * (f // 2) + j, 128 * lax.rem(f, 2)

    def chunk_copy(idx, own, way):
        j, f = unit(idx // CHUNKS)
        r = CHUNK_ROWS * lax.rem(idx, CHUNKS)
        target = cols.at[j, pl.ds(pl.multiple_of(128 * f + r, CHUNK_ROWS), CHUNK_ROWS)]
        if own:
            block, offset = home(j, f)
            source = rows.at[block, pl.ds(pl.multiple_of(offset + r, CHUNK_ROWS), CHUNK_ROWS)]
        else:
            source = target
        dz = onward if way == 0 else -onward
        return remote(source, target, send.at[way, idx], recv.at[idx], at(dz=dz))

    def stream(idx):
        @pl.when(place == 0)
        def _():
            chunk_copy(idx, True, 0).start()
            chunk_copy(idx, True, 1).start()

        @pl.when(place >= 1)
        def _():
            copy = chunk_copy(idx, False, 0)
            copy.wait_recv()

            @pl.when(place <= 5)
            def _():
                copy.start()

    def serve(idx):
        n = idx + behind

        @pl.when(idx == 8 * (1 - relay))
        def _():
            for copy in ring_copies:
                copy.wait_recv()
            mean, update, weight = merge(ring[...])
            for row, value in enumerate((mean, update, weight, weight)):
                means[0, row : row + 1, :] = value
            update_ref[...] = update * (1.0 / 8192.0**0.5)
            for copy in mean_copies:
                copy.start()

        @pl.when(n == 32)
        def _():
            to_down(0).wait_recv()
            to_up(0).wait_recv()
            share(0, 1).start()
            share(0, 2).start()
            across().wait_recv()
            to_up(1).start()
            to_down(1).start()
            share(1, 0).start()
            half_down(0).start()
            half_up(0).start()

        @pl.when(n == 32 + 5 * relay)
        def _():
            share(0, 1).wait_recv()
            share(0, 2).wait_recv()
            share(1, 0).wait_recv()
            for copy in mean_copies:
                copy.wait_recv()

        @pl.when(n == 66)
        def _():
            to_down(1).wait_recv()
            to_up(1).wait_recv()
            share(1, 1).start()
            share(1, 2).start()
            half_down(1).start()
            half_up(1).start()

        @pl.when(n == 72)
        def _():
            share(1, 1).wait_recv()
            share(1, 2).wait_recv()

        @pl.when(n == 80)
        def _():
            half_down(0).wait_recv()
            half_up(0).wait_recv()
            share(0, 3).start()

        @pl.when(n == 80 + 5 * relay)
        def _():
            share(0, 3).wait_recv()

        @pl.when(n == 108)
        def _():
            half_down(1).wait_recv()
            half_up(1).wait_recv()
            share(1, 3).start()

        @pl.when(n == 116)
        def _():
            share(1, 3).wait_recv()

    def part_copy(f, k):
        slot = 4 * f + 2 * xh + core
        device = {"smp": (lax.rem(xl + k // 2, 2) * NZ + z) * 2 + lax.rem(core + k, 2), "par": xl * NY + y}
        block = pl.ds(pl.multiple_of(256 * k, 256), 256)
        return remote(part.at[f, block], landed.at[slot], part_send.at[4 * f + k], part_recv.at[slot], device)

    def stays(k):
        return jnp.logical_and(xl == xh, k == 0)

    def compute(idx):
        t = idx + behind - COMPUTE_AT
        u, k = t // CHUNKS, lax.rem(t, CHUNKS)
        j, f = unit(u)
        tile = pl.ds(pl.multiple_of(128 * k, 128), 128)

        @pl.when(jnp.logical_and(t >= 0, t < STEPS))
        def _():
            @pl.when(k == 0)
            def _():
                def convert(block):
                    high, low = split(block - means[j, 0:1, :])
                    col_hi[...] = high
                    col_lo[...] = low

                @pl.when(place == 0)
                def _():
                    block, offset = home(j, f)
                    convert(rows[block, pl.ds(pl.multiple_of(offset, 128), 128), :])

                @pl.when(place != 0)
                def _():
                    convert(cols[j, pl.ds(pl.multiple_of(128 * f, 128), 128), :])

            @pl.when(f == 0)
            def _():
                inner = pl.ds(pl.multiple_of(128 * lax.rem(k, 2), 128), 128)
                high, low = split(rows[4 * (k // 2) + j, inner, :] - means[j, 0:1, :])
                row_hi[j, tile, :] = high
                row_lo[j, tile, :] = low

            total = product(row_hi[j, tile, :], col_hi[...])
            total += product(row_hi[j, tile, :], col_lo[...])
            total += product(row_lo[j, tile, :], col_hi[...])

            @pl.when(j == 0)
            def _():
                part[f, tile, :] = total

            @pl.when(j != 0)
            def _():
                part[f, tile, :] += total

            @pl.when(jnp.logical_and(j == 3, lax.rem(k, 2) == 1))
            def _():
                @pl.when(stays(k // 2))
                def _():
                    landed[4 * f + 2 * xh + core] = part[f, 0:256, :]

                @pl.when(jnp.logical_not(stays(k // 2)))
                def _():
                    part_copy(f, k // 2).start()

    @pl.when(place == 0)
    def _():
        @pl.loop(0, EARLY)
        def _(idx):
            stream(idx)

    to_up(0).start()
    to_down(0).start()
    x = rows[0]
    mean = jnp.sum(x, axis=0, keepdims=True) * (1.0 / x.shape[0])
    coef = coef_ref[...]
    weighted = lax.dot_general(
        jnp.broadcast_to(coef, (8, coef.shape[1])), x - mean, (((1,), (0,)), ((), ())),
        precision=lax.Precision.HIGHEST, preferred_element_type=jnp.float32,
    )
    weight = jnp.broadcast_to(jnp.sum(coef, axis=1, keepdims=True), mean.shape)
    near[0, 0:1, :] = mean
    near[0, 1:2, :] = weighted[0:1, :]
    near[0, 2:3, :] = weight
    near[0, 3:4, :] = weight
    for copy in near_copies:
        copy.start()
    across().start()
    share(0, 0).start()
    for copy in near_copies:
        copy.wait_recv()
    merged = merge(near[...])
    for row, value in enumerate(merged + (merged[2],)):
        ring[0, row : row + 1, :] = value
    for copy in ring_copies:
        copy.start()
    share(0, 0).wait_recv()

    @pl.loop(0, STEPS)
    def _(idx):
        serve(idx)

        @pl.when(idx >= EARLY * (1 - relay))
        def _():
            stream(idx)

        compute(idx)

    @pl.loop(STEPS, STEPS + COMPUTE_AT)
    def _(idx):
        serve(idx)
        compute(idx)

    for f in range(4):
        for source_xh in range(2):
            for source_core in range(2):
                slot = 4 * f + 2 * source_xh + source_core
                own = jnp.logical_and(jnp.logical_and(xl == xh, xh == source_xh), core == source_core)

                @pl.when(jnp.logical_not(own))
                def _():
                    remote(part.at[0, pl.ds(0, 256)], landed.at[slot], part_send.at[0], part_recv.at[slot], at(dc=1)).wait_recv()

        for source_core in range(2):
            first = 512 * (1 - source_core) + 256 * ((source_core + f // 2) % 2) + 128 * (f % 2)
            gram_ref[:, first : first + 128] = (landed[4 * f + source_core] + landed[4 * f + 2 + source_core]) * (1.0 / 8192.0)

    for copy in near_copies + ring_copies + mean_copies:
        copy.wait_send()
    for copy in (across(), to_up(0), to_down(0), to_up(1), to_down(1), half_down(0), half_up(0), half_down(1), half_up(1)):
        copy.wait_send()
    for g in range(2):
        for j in range(4):
            share(g, j).wait_send()

    @pl.loop(0, STEPS)
    def _(idx):
        @pl.when(place <= 5)
        def _():
            chunk_copy(idx, False, 0).wait_send()

        @pl.when(place == 0)
        def _():
            chunk_copy(idx, True, 1).wait_send()

    @pl.loop(0, 4)
    def _(f):
        for k in range(4):
            @pl.when(jnp.logical_not(stays(k)))
            def _():
                part_copy(f, k).wait_send()


def local(log_derivs, coefficients):
    count, width = log_derivs.shape
    dma = pltpu.SemaphoreType.DMA
    f32, bf16 = jnp.float32, jnp.bfloat16
    gram, update = pl.pallas_call(
        kernel,
        out_shape=(jax.ShapeDtypeStruct((count, width), f32), jax.ShapeDtypeStruct((1, width), f32)),
        in_specs=[pl.BlockSpec(memory_space=pl.ANY), pl.BlockSpec(memory_space=pltpu.VMEM)],
        out_specs=(pl.BlockSpec(memory_space=pltpu.VMEM), pl.BlockSpec(memory_space=pltpu.VMEM)),
        scratch_shapes=[
            pltpu.VMEM((16, count, width), f32),
            pltpu.VMEM((NY, 2 * count, width), f32),
            pltpu.VMEM((4, 4 * count, count // 2), f32),
            pltpu.VMEM((16, count, count // 2), f32),
            pltpu.VMEM((NY, 4 * count, width), bf16),
            pltpu.VMEM((NY, 4 * count, width), bf16),
            pltpu.VMEM((count // 2, width), bf16),
            pltpu.VMEM((count // 2, width), bf16),
            pltpu.VMEM((4, 4, width), f32),
            pltpu.VMEM((NZ, 4, width), f32),
            pltpu.VMEM((NY, 4, width), f32),
            dma(()), dma((3,)), dma((3,)), dma((NZ - 1,)), dma((NZ - 1,)), dma((3,)), dma((3,)),
            dma((8,)), dma((16,)), dma((4,)), dma((4,)), dma((8,)),
            dma((2, STEPS)), dma((STEPS,)), dma((16,)), dma((16,)),
        ],
        compiler_params=pltpu.CompilerParams(collective_id=0, has_side_effects=True, vmem_limit_bytes=60 * 2**20),
    )(log_derivs, coefficients.reshape(1, count))
    start = lax.axis_index("smp") * (width // lax.axis_size("smp"))
    return gram, lax.dynamic_slice(update.reshape(width), (start,), (width // lax.axis_size("smp"),))


def solution(mesh):
    placed = (P("smp", "par"), P("smp"))
    return jax.shard_map(
        local,
        mesh=mesh,
        in_specs=placed,
        out_specs=(P("smp", "par"), P(("par", "smp"))),
        check_vma=False,
    )
```

```python
import functools

import jax
import jax.numpy as jnp
from jax import lax
from jax.experimental import pallas as pl
from jax.experimental.pallas import tpu as pltpu
from jax.sharding import PartitionSpec as P

MESH = pl.DeviceIdType.MESH
NZ, NY = 8, 4
UNITS = 16
CHUNK_ROWS = 16
CHUNKS = 128 // CHUNK_ROWS
STEPS = UNITS * CHUNKS
HOP = 5
COMPUTE_AT = 38
EARLY = 8


def merge(stats):
    count = stats.shape[0]
    mean = jnp.sum(stats[:, 0:1, :], axis=0) * (1.0 / count)
    shift = stats[:, 0:1, :] - mean[None]
    update = jnp.sum(stats[:, 1:2, :] + stats[:, 2:3, :] * shift, axis=0)
    weight = jnp.sum(stats[:, 2:3, :], axis=0)
    return mean, update, weight


def split(values):
    high = values.astype(jnp.bfloat16)
    low = (values - high.astype(jnp.float32)).astype(jnp.bfloat16)
    return high, low


def product(left, right):
    return lax.dot_general(left, right, (((1,), (1,)), ((), ())), preferred_element_type=jnp.float32)


def kernel(
    x_ref, coef_ref, gram_ref, update_ref,
    rows, cols, part, landed, row_hi, row_lo, col_hi, col_lo, near, ring, means,
    load_sem, near_send, near_recv, ring_send, ring_recv, mean_send, mean_recv,
    row_send, row_recv, half_send, half_recv, share_send, send, recv, part_send, part_recv,
):
    smp, par = lax.axis_index("smp"), lax.axis_index("par")
    core, z, xl = lax.rem(smp, 2), lax.rem(smp // 2, NZ), smp // (2 * NZ)
    y, xh = lax.rem(par, NY), par // NY
    place = lax.rem((1 - 2 * core) * (z - 2 * y - 1) + 3 * NZ - core, NZ)
    onward = 1 - 2 * core
    relay = (place + 7) // 8
    behind = HOP * (place - 6 * (place // 7))

    def at(dz=0, dy=0, dc=0, dxl=0, dxh=0):
        zz, yy = lax.rem(z + dz + NZ, NZ), lax.rem(y + dy + NY, NY)
        cc, ll, hh = lax.rem(core + dc, 2), lax.rem(xl + dxl, 2), lax.rem(xh + dxh, 2)
        return {"smp": (ll * NZ + zz) * 2 + cc, "par": hh * NY + yy}

    def remote(src, dst, s_sem, r_sem, device):
        return pltpu.make_async_remote_copy(
            src_ref=src, dst_ref=dst, send_sem=s_sem, recv_sem=r_sem, device_id=device, device_id_type=MESH
        )

    load = pltpu.make_async_copy(x_ref, rows.at[0], load_sem)
    load.start()
    barrier = pltpu.get_barrier_semaphore()
    for dz in range(1, NZ):
        pl.semaphore_signal(barrier, inc=1, device_id=at(dz=dz), device_id_type=MESH)
    for dy in range(1, NY):
        pl.semaphore_signal(barrier, inc=1, device_id=at(dy=dy), device_id_type=MESH)
    for b in range(1, 8):
        pl.semaphore_signal(barrier, inc=1, device_id=at(dc=b % 2, dxl=b // 2 % 2, dxh=b // 4), device_id_type=MESH)
    load.wait()
    pl.semaphore_wait(barrier, NZ + NY + 8 - 3)

    near_copies = [
        remote(near.at[0], near.at[b], near_send.at[b - 1], near_recv.at[b - 1], at(dc=b % 2, dxl=b // 2))
        for b in range(1, 4)
    ]
    ring_copies = [
        remote(ring.at[0], ring.at[NZ - dz], ring_send.at[dz - 1], ring_recv.at[NZ - dz - 1], at(dz=dz))
        for dz in range(1, NZ)
    ]
    mean_copies = [
        remote(means.at[0], means.at[slot], mean_send.at[slot - 1], mean_recv.at[slot - 1], at(dy=dy))
        for slot, dy in ((2, 1), (1, -1), (3, 2))
    ]

    def to_up(g):
        return remote(rows.at[8 * g], rows.at[8 * g + 2], row_send.at[4 * g], row_recv.at[4 * g + 2], at(dy=1))

    def to_down(g):
        return remote(rows.at[8 * g], rows.at[8 * g + 1], row_send.at[4 * g + 1], row_recv.at[4 * g + 1], at(dy=-1))

    def half_down(g):
        top = pl.ds(0, 128)
        return remote(rows.at[8 * g + 1, top], rows.at[8 * g + 3, top], half_send.at[2 * g], half_recv.at[2 * g], at(dy=-1))

    def half_up(g):
        low = pl.ds(128, 128)
        return remote(rows.at[8 * g + 2, low], rows.at[8 * g + 3, low], half_send.at[2 * g + 1], half_recv.at[2 * g + 1], at(dy=1))

    def across():
        return remote(rows.at[0], rows.at[8], row_send.at[2], row_recv.at[0], at(dxl=1))

    def share(g, j):
        slot = 4 * g + j
        return remote(rows.at[8 * g + j], rows.at[8 * g + 4 + j], share_send.at[slot], row_recv.at[8 + slot], at(dc=1))

    def unit(u):
        q, v = u // 4, lax.rem(u, 4)
        third, fourth = (q // 2) * (1 - lax.rem(q, 2)), (q // 2) * lax.rem(q, 2)
        first = 1 - q // 2
        j = first * q + third * (2 + v // 2) + fourth * (2 + lax.rem(v, 2))
        f = first * v + third * lax.rem(v, 2) + fourth * (2 + v // 2)
        return j, f

    def home(j, f):
        return 4 * (f // 2) + j, 128 * lax.rem(f, 2)

    def chunk_copy(idx, own, way):
        j, f = unit(idx // CHUNKS)
        r = CHUNK_ROWS * lax.rem(idx, CHUNKS)
        target = cols.at[j, pl.ds(pl.multiple_of(128 * f + r, CHUNK_ROWS), CHUNK_ROWS)]
        if own:
            block, offset = home(j, f)
            source = rows.at[block, pl.ds(pl.multiple_of(offset + r, CHUNK_ROWS), CHUNK_ROWS)]
        else:
            source = target
        dz = onward if way == 0 else -onward
        return remote(source, target, send.at[way], recv.at[idx], at(dz=dz))

    def stream(idx):
        @pl.when(place == 0)
        def _():
            chunk_copy(idx, True, 0).start()
            chunk_copy(idx, True, 1).start()

        @pl.when(place >= 1)
        def _():
            copy = chunk_copy(idx, False, 0)
            copy.wait_recv()

            @pl.when(place <= 5)
            def _():
                copy.start()

    def serve(idx):
        n = idx + behind

        @pl.when(idx == 8 * (1 - relay))
        def _():
            for copy in ring_copies:
                copy.wait_recv()
            mean, update, weight = merge(ring[...])
            for row, value in enumerate((mean, update, weight, weight)):
                means[0, row : row + 1, :] = value
            update_ref[...] = update * (1.0 / 8192.0**0.5)
            for copy in mean_copies:
                copy.start()

        @pl.when(n == 32)
        def _():
            to_down(0).wait_recv()
            to_up(0).wait_recv()
            share(0, 1).start()
            share(0, 2).start()
            across().wait_recv()
            to_up(1).start()
            to_down(1).start()
            share(1, 0).start()
            half_down(0).start()
            half_up(0).start()

        @pl.when(n == 32 + 5 * relay)
        def _():
            share(0, 1).wait_recv()
            share(0, 2).wait_recv()
            share(1, 0).wait_recv()
            for copy in mean_copies:
                copy.wait_recv()

        @pl.when(n == 66)
        def _():
            to_down(1).wait_recv()
            to_up(1).wait_recv()
            share(1, 1).start()
            share(1, 2).start()
            half_down(1).start()
            half_up(1).start()

        @pl.when(n == 72)
        def _():
            share(1, 1).wait_recv()
            share(1, 2).wait_recv()

        @pl.when(n == 80)
        def _():
            half_down(0).wait_recv()
            half_up(0).wait_recv()
            share(0, 3).start()

        @pl.when(n == 80 + 5 * relay)
        def _():
            share(0, 3).wait_recv()

        @pl.when(n == 108)
        def _():
            half_down(1).wait_recv()
            half_up(1).wait_recv()
            share(1, 3).start()

        @pl.when(n == 116)
        def _():
            share(1, 3).wait_recv()

    def part_copy(f, k):
        slot = 4 * f + 2 * xh + core
        device = {"smp": (lax.rem(xl + k // 2, 2) * NZ + z) * 2 + lax.rem(core + k, 2), "par": xl * NY + y}
        block = pl.ds(pl.multiple_of(256 * k, 256), 256)
        return remote(part.at[f, block], landed.at[slot], part_send.at[4 * f + k], part_recv.at[slot], device)

    def stays(k):
        return jnp.logical_and(xl == xh, k == 0)

    def compute(idx):
        t = idx + behind - COMPUTE_AT
        u, r = t // CHUNKS, lax.rem(t, CHUNKS)
        k = r // 2
        j, f = unit(u)
        tile = pl.ds(pl.multiple_of(256 * k, 256), 256)

        @pl.when(jnp.logical_and(jnp.logical_and(t >= 0, t < STEPS), lax.rem(r, 2) == 0))
        def _():
            @pl.when(k == 0)
            def _():
                def convert(block):
                    high, low = split(block - means[j, 0:1, :])
                    col_hi[...] = high
                    col_lo[...] = low

                @pl.when(place == 0)
                def _():
                    block, offset = home(j, f)
                    convert(rows[block, pl.ds(pl.multiple_of(offset, 128), 128), :])

                @pl.when(place != 0)
                def _():
                    convert(cols[j, pl.ds(pl.multiple_of(128 * f, 128), 128), :])

            @pl.when(f == 0)
            def _():
                high, low = split(rows[4 * k + j] - means[j, 0:1, :])
                row_hi[j, tile, :] = high
                row_lo[j, tile, :] = low

            total = product(row_hi[j, tile, :], col_hi[...])
            total += product(row_hi[j, tile, :], col_lo[...])
            total += product(row_lo[j, tile, :], col_hi[...])

            @pl.when(j == 0)
            def _():
                part[f, tile, :] = total

            @pl.when(j != 0)
            def _():
                part[f, tile, :] += total

            @pl.when(j == 3)
            def _():
                @pl.when(stays(k))
                def _():
                    landed[4 * f + 2 * xh + core] = part[f, 0:256, :]

                @pl.when(jnp.logical_not(stays(k)))
                def _():
                    part_copy(f, k).start()

    @pl.when(place == 0)
    def _():
        @pl.loop(0, EARLY)
        def _(idx):
            stream(idx)

    to_up(0).start()
    to_down(0).start()
    x = rows[0]
    mean = jnp.sum(x, axis=0, keepdims=True) * (1.0 / x.shape[0])
    coef = coef_ref[...]
    weighted = lax.dot_general(
        jnp.broadcast_to(coef, (8, coef.shape[1])), x - mean, (((1,), (0,)), ((), ())),
        precision=lax.Precision.HIGHEST, preferred_element_type=jnp.float32,
    )
    weight = jnp.broadcast_to(jnp.sum(coef, axis=1, keepdims=True), mean.shape)
    near[0, 0:1, :] = mean
    near[0, 1:2, :] = weighted[0:1, :]
    near[0, 2:3, :] = weight
    near[0, 3:4, :] = weight
    for copy in near_copies:
        copy.start()
    across().start()
    share(0, 0).start()
    for copy in near_copies:
        copy.wait_recv()
    merged = merge(near[...])
    for row, value in enumerate(merged + (merged[2],)):
        ring[0, row : row + 1, :] = value
    for copy in ring_copies:
        copy.start()
    share(0, 0).wait_recv()

    @pl.loop(0, STEPS)
    def _(idx):
        serve(idx)

        @pl.when(idx >= EARLY * (1 - relay))
        def _():
            stream(idx)

        compute(idx)

    @pl.loop(STEPS, STEPS + COMPUTE_AT - behind)
    def _(idx):
        serve(idx)
        compute(idx)

    for f in range(4):
        for source_xh in range(2):
            for source_core in range(2):
                slot = 4 * f + 2 * source_xh + source_core
                own = jnp.logical_and(jnp.logical_and(xl == xh, xh == source_xh), core == source_core)

                @pl.when(jnp.logical_not(own))
                def _():
                    remote(part.at[0, pl.ds(0, 256)], landed.at[slot], part_send.at[0], part_recv.at[slot], at(dc=1)).wait_recv()

        for source_core in range(2):
            first = 512 * (1 - source_core) + 256 * ((source_core + f // 2) % 2) + 128 * (f % 2)
            gram_ref[:, first : first + 128] = (landed[4 * f + source_core] + landed[4 * f + 2 + source_core]) * (1.0 / 8192.0)

    for copy in near_copies + ring_copies + mean_copies:
        copy.wait_send()
    for copy in (across(), to_up(0), to_down(0), to_up(1), to_down(1), half_down(0), half_up(0), half_down(1), half_up(1)):
        copy.wait_send()
    for g in range(2):
        for j in range(4):
            share(g, j).wait_send()

    @pl.when(place <= 5)
    def _():
        remote(cols, cols, send.at[0], recv.at[0], at(dz=onward)).wait_send()

    @pl.when(place == 0)
    def _():
        remote(cols, cols, send.at[1], recv.at[0], at(dz=onward)).wait_send()

    @pl.loop(0, 4)
    def _(f):
        for k in range(4):
            @pl.when(jnp.logical_not(stays(k)))
            def _():
                part_copy(f, k).wait_send()


def local(log_derivs, coefficients):
    count, width = log_derivs.shape
    dma = pltpu.SemaphoreType.DMA
    f32, bf16 = jnp.float32, jnp.bfloat16
    gram, update = pl.pallas_call(
        kernel,
        out_shape=(jax.ShapeDtypeStruct((count, width), f32), jax.ShapeDtypeStruct((1, width), f32)),
        in_specs=[pl.BlockSpec(memory_space=pl.ANY), pl.BlockSpec(memory_space=pltpu.VMEM)],
        out_specs=(pl.BlockSpec(memory_space=pltpu.VMEM), pl.BlockSpec(memory_space=pltpu.VMEM)),
        scratch_shapes=[
            pltpu.VMEM((16, count, width), f32),
            pltpu.VMEM((NY, 2 * count, width), f32),
            pltpu.VMEM((4, 4 * count, count // 2), f32),
            pltpu.VMEM((16, count, count // 2), f32),
            pltpu.VMEM((NY, 4 * count, width), bf16),
            pltpu.VMEM((NY, 4 * count, width), bf16),
            pltpu.VMEM((count // 2, width), bf16),
            pltpu.VMEM((count // 2, width), bf16),
            pltpu.VMEM((4, 4, width), f32),
            pltpu.VMEM((NZ, 4, width), f32),
            pltpu.VMEM((NY, 4, width), f32),
            dma(()), dma((3,)), dma((3,)), dma((NZ - 1,)), dma((NZ - 1,)), dma((3,)), dma((3,)),
            dma((8,)), dma((16,)), dma((4,)), dma((4,)), dma((8,)),
            dma((2,)), dma((STEPS,)), dma((16,)), dma((16,)),
        ],
        compiler_params=pltpu.CompilerParams(collective_id=0, has_side_effects=True, vmem_limit_bytes=60 * 2**20),
    )(log_derivs, coefficients.reshape(1, count))
    start = lax.axis_index("smp") * (width // lax.axis_size("smp"))
    return gram, lax.dynamic_slice(update.reshape(width), (start,), (width // lax.axis_size("smp"),))


def solution(mesh):
    placed = (P("smp", "par"), P("smp"))
    return jax.shard_map(
        local,
        mesh=mesh,
        in_specs=placed,
        out_specs=(P("smp", "par"), P(("par", "smp"))),
        check_vma=False,
    )
```
